32 devices in a mesh: lon: 8 (over z, core), head: 4 (over y, x).
Axes of the slice: x: 2, y: 2, z: 4, core: 2. Of those that a mesh axis runs over, the one named last changes fastest.
Arguments:
- image_tokens: bfloat16 [64, 128, 3072], P(None, 'lon'), may hold values from -6 to 6
- conditioning: bfloat16 [3072], replicated, may hold values from -6 to 6
- mod_weight: bfloat16 [3072, 3, 3072], P(('lon', 'head')), may hold values from -0.21875 to 0.21875
- mod_bias: bfloat16 [3, 3072], replicated, may hold values from -3 to 3
- qkv_weight: bfloat16 [3072, 3, 3072], P('lon', None, 'head'), may hold values from -0.109375 to 0.109375
- qkv_bias: bfloat16 [3, 3072], P(None, 'head'), may hold values from -3 to 3
- q_gain: float32 [128], replicated, may hold values from 0.5 to 12
- k_gain: float32 [128], replicated, may hold values from 0.5 to 12
- text_kv: bfloat16 [2, 512, 3072], P(None, 'lon', 'head'), may hold values from -6 to 6
- proj_weight: bfloat16 [3072, 3072], P('lon', 'head'), may hold values from -0.109375 to 0.109375
- proj_bias: bfloat16 [3072], replicated, may hold values from -3 to 3
Outputs:
- block_output: bfloat16 [64, 128, 3072], P(None, 'lon', 'head')
The draws below stay inside these ranges and needn't reach their ends.
All inputs are finite; a program needn't handle non-finite values.
Results may differ from the reference program's by a relative error of at most 0.0109.
The reference program's roundings to bfloat16 on the way count: a program that leaves them out, or rounds other values in their place, can miss the bound.
Values may be sent and summed in bfloat16 or wider, within the bound.
A program may use at most 128 MiB of HBM per device.

```python
import math
import jax
import jax.numpy as jnp
from jax import lax

D = 3072
HEADS = 24
HD = 128
TXT = 512
LAT = 64
COLS = 16
RADIUS = 15
QROWS = 16
LON = 128


def draw_gain_vector(key):
    return jnp.exp(jax.random.uniform(key, (HD,), jnp.float32, math.log(0.5), math.log(2.0)))


def draw_q_gain(key, part):
    return draw_gain_vector(jax.random.fold_in(key, 101))


def draw_k_gain(key, part):
    return draw_gain_vector(jax.random.fold_in(key, 202))


def raised(values, rng, source, target, parts, factor):
    def block_of(position):
        return (jnp.arange(values.shape[position]) // (values.shape[position] // parts)).reshape((-1,) + (1,) * (values.ndim - 1 - position))

    near = jax.random.permutation(rng, parts)[block_of(target)]
    other_side = (block_of(target) + parts // 2) % parts
    return jnp.where((block_of(source) == near) | (block_of(source) == other_side), factor * values, values)


def block_levels(stream_key, extent, split, low, top_value):
    factor_of, own = 1.0, jax.random.fold_in(stream_key, 6)
    for dim, shards_of in split:
        draws = jnp.exp(jax.random.uniform(jax.random.fold_in(own, dim), (shards_of,), jnp.float32, low / len(split), top_value / len(split)))
        factor_of = factor_of * jnp.repeat(draws, extent[dim] // shards_of).reshape([-1 if axis == dim else 1 for axis in range(len(extent))])
    return factor_of


def bell_draw(rng, extent, width, reach, shards=(), kind=jnp.bfloat16):
    values = width * jax.random.normal(rng, extent, jnp.float32)
    if shards:
        values = values * block_levels(rng, extent, shards, -0.22, 0.18)
    return jnp.clip(values, -reach, reach).astype(kind)


def gaussian_with(key, shape, width, bound, pieces, heavy, kind=jnp.bfloat16):
    values = width * jax.random.normal(key, shape, jnp.float32)
    if pieces:
        values = values * block_levels(key, shape, pieces, -0.22, 0.18)
    return jnp.clip(raised(values, jax.random.fold_in(key, 3), *heavy), -bound, bound).astype(kind)


def setup_inputs(seed: int = 0) -> dict:
    key_of = jax.random.split(jax.random.key(seed), 12)
    return {
        "image_tokens": bell_draw(key_of[0], (LAT, LON, D), 1.0, 6.0, ((1, 8),)),
        "conditioning": bell_draw(key_of[1], (D,), 1.0, 6.0),
        "mod_weight": gaussian_with(key_of[2], (D, 3, D), D ** -0.5, 0.21875, ((0, 32),), (0, 2, 32, 2.75)),
        "mod_bias": bell_draw(key_of[3], (3, D), 0.5, 3.0),
        "qkv_weight": bell_draw(key_of[4], (D, 3, HEADS * HD), D ** -0.5, 0.109375, ((0, 8), (2, 4))),
        "qkv_bias": bell_draw(key_of[5], (3, HEADS * HD), 0.5, 3.0, ((1, 4),)),
        "q_gain": draw_q_gain(jax.random.fold_in(key_of[11], 71), 0),
        "k_gain": draw_k_gain(jax.random.fold_in(key_of[11], 71), 0),
        "text_kv": bell_draw(key_of[8], (2, TXT, HEADS * HD), 1.0, 6.0, ((1, 8), (2, 4))),
        "proj_weight": bell_draw(key_of[9], (HEADS * HD, D), (HEADS * HD) ** -0.5, 0.109375, ((0, 8), (1, 4))),
        "proj_bias": bell_draw(key_of[10], (D,), 0.5, 3.0),
    }


def rms_scale(entries, gain):
    mean_square = lax.optimization_barrier(jnp.mean(entries * entries, axis=-1, keepdims=True))
    return entries * lax.rsqrt(mean_square + 1e-06) * gain

def window_mask(row_first, q_rows, q_cols, k_rows, k_cols, lat_total):
    query_index = jnp.arange(q_rows * q_cols, dtype=jnp.int32)
    key_index = jnp.arange(k_rows * k_cols, dtype=jnp.int32)
    query_row = (query_index // q_cols)[:, None]
    query_col = (query_index % q_cols)[:, None]
    key_row = (key_index // k_cols)[None, :]
    key_col = (key_index % k_cols)[None, :]
    global_row = row_first + key_row - RADIUS
    near_rows = jnp.abs(key_row - RADIUS - query_row) <= RADIUS
    near_cols = jnp.abs(key_col - RADIUS - query_col) <= RADIUS
    inside = (global_row >= 0) & (global_row < lat_total)
    return near_rows & near_cols & inside

def attend(queries, key_block, value_block, text_keys, text_values, row_first):
    q_rows, q_cols, heads_here, head_dim = queries.shape
    k_rows, k_cols = (key_block.shape[0], key_block.shape[1])
    flat_query = queries.reshape(q_rows * q_cols, heads_here, head_dim).astype(jnp.float32)
    flat_keys = key_block.reshape(k_rows * k_cols, heads_here, head_dim).astype(jnp.float32)
    flat_values = value_block.reshape(k_rows * k_cols, heads_here, head_dim).astype(jnp.float32)
    factor = 1.0 / math.sqrt(head_dim)
    image_scores = jnp.einsum('qhd,khd->hqk', flat_query, flat_keys) * factor
    text_scores = jnp.einsum('qhd,khd->hqk', flat_query, text_keys.astype(jnp.float32)) * factor
    allowed = window_mask(row_first, q_rows, q_cols, k_rows, k_cols, LAT)
    image_scores = jnp.where(allowed[None], image_scores, -jnp.inf)
    highest = jnp.maximum(lax.optimization_barrier(jnp.max(image_scores, axis=2, keepdims=True)), lax.optimization_barrier(jnp.max(text_scores, axis=2, keepdims=True)))
    image_exp = jnp.exp(image_scores - highest)
    text_exp = jnp.exp(text_scores - highest)
    normaliser = lax.optimization_barrier(jnp.sum(image_exp, axis=2, keepdims=True)) + lax.optimization_barrier(jnp.sum(text_exp, axis=2, keepdims=True))
    image_probs = (image_exp / normaliser).astype(jnp.bfloat16)
    text_probs = (text_exp / normaliser).astype(jnp.bfloat16)
    combined = jnp.einsum('hqk,khd->qhd', image_probs.astype(jnp.float32), flat_values)
    combined = combined + jnp.einsum('hqk,khd->qhd', text_probs.astype(jnp.float32), text_values.astype(jnp.float32))
    return combined.astype(jnp.bfloat16).reshape(q_rows, q_cols, heads_here * head_dim)

def reference(image_tokens, conditioning, mod_weight, mod_bias, qkv_weight, qkv_bias, q_gain, k_gain, text_kv, proj_weight, proj_bias):
    model_width = D
    inner_width = HEADS * HD
    silu_cond = jax.nn.silu(conditioning.astype(jnp.float32))
    modulation = jnp.dot(silu_cond, mod_weight.reshape(model_width, 3 * model_width).astype(jnp.float32), precision=lax.Precision.HIGHEST)
    modulation = modulation.reshape(3, model_width) + mod_bias.astype(jnp.float32)
    shift_row, scale_row, gate_row = (modulation[0], modulation[1], modulation[2])
    token_values = image_tokens.astype(jnp.float32).reshape(LAT * LON, model_width)
    average = lax.optimization_barrier(jnp.mean(token_values, axis=1, keepdims=True))
    centred = token_values - average
    variance = lax.optimization_barrier(jnp.mean(centred * centred, axis=1, keepdims=True))
    modulated = ((1.0 + scale_row) * (centred * lax.rsqrt(variance + 1e-06)) + shift_row).astype(jnp.bfloat16)
    projected = jnp.dot(modulated, qkv_weight.reshape(model_width, 3 * inner_width), preferred_element_type=jnp.float32)
    projected = projected.reshape(LAT * LON, 3, inner_width) + qkv_bias.astype(jnp.float32)
    queries = rms_scale(projected[:, 0].reshape(LAT, LON, HEADS, HD), q_gain).astype(jnp.bfloat16)
    keys_normed = rms_scale(projected[:, 1].reshape(LAT, LON, HEADS, HD), k_gain).astype(jnp.bfloat16)
    values_image = projected[:, 2].reshape(LAT, LON, HEADS, HD).astype(jnp.bfloat16)

    def widen(field):
        wrapped = jnp.concatenate([field[:, LON - RADIUS:], field, field[:, :RADIUS]], axis=1)
        return jnp.pad(wrapped, ((RADIUS, RADIUS), (0, 0), (0, 0), (0, 0)))
    padded_keys = widen(keys_normed)
    padded_values = widen(values_image)
    text_keys = text_kv[0].reshape(TXT, HEADS, HD)
    text_values = text_kv[1].reshape(TXT, HEADS, HD)
    col_blocks = LON // COLS
    block_count = LAT // QROWS * col_blocks
    zero_index = jnp.int32(0)

    def one_block(block_index):
        row_first = block_index // col_blocks * QROWS
        col_first = block_index % col_blocks * COLS
        query_block = lax.dynamic_slice(queries, (row_first, col_first, zero_index, zero_index), (QROWS, COLS, HEADS, HD))
        key_block = lax.dynamic_slice(padded_keys, (row_first, col_first, zero_index, zero_index), (QROWS + 2 * RADIUS, COLS + 2 * RADIUS, HEADS, HD))
        value_block = lax.dynamic_slice(padded_values, (row_first, col_first, zero_index, zero_index), (QROWS + 2 * RADIUS, COLS + 2 * RADIUS, HEADS, HD))
        return attend(query_block, key_block, value_block, text_keys, text_values, row_first)
    blocks = lax.map(one_block, jnp.arange(block_count, dtype=jnp.int32))
    blocks = blocks.reshape(LAT // QROWS, col_blocks, QROWS, COLS, inner_width)
    attended = jnp.transpose(blocks, (0, 2, 1, 3, 4)).reshape(LAT * LON, inner_width)
    out_sum = jnp.dot(attended, proj_weight, preferred_element_type=jnp.float32) + proj_bias.astype(jnp.float32)
    block_output = (token_values + gate_row * out_sum).astype(jnp.bfloat16)
    return block_output.reshape(LAT, LON, model_width)
```

```python
import functools
import math

import jax
import jax.numpy as jnp
from jax import lax
from jax.experimental import pallas as pl
from jax.experimental.pallas import tpu as pltpu
from jax.sharding import PartitionSpec as P

RADIUS = 15
QROWS = 16
VMEM_LIMIT = 63 * 1024 * 1024
MESH = pl.DeviceIdType.MESH


def kernel(
    sizes,
    x_hbm,
    part_ref,
    mod_bias_ref,
    w_hbm,
    qkv_bias_ref,
    q_gain_ref,
    k_gain_ref,
    text_hbm,
    proj_hbm,
    proj_bias_ref,
    out_hbm,
    xm,
    xh,
    wbuf,
    pbuf,
    tbuf,
    kv_own,
    kv_inner,
    kv_outer,
    q_buf,
    ag,
    img,
    near,
    pa,
    pb,
    mod,
    sem_pa_s,
    sem_pa_r,
    sem_pb_s,
    sem_pb_r,
    sem_w_s,
    sem_w_r,
    sem_p_s,
    sem_p_r,
    sem_t_s,
    sem_t_r,
    sem_h_s,
    sem_h_r,
    sem_f_s,
    sem_f_r,
    sem_kv_s,
    sem_kv_r,
    sem_a_s,
    sem_a_r,
    sem_x,
    sem_img,
    sem_out,
):
    lons, heads, cols, head_dim = sizes
    line = lons // 2
    lon, head = lax.axis_index("lon"), lax.axis_index("head")
    z, core = lon // 2, lax.rem(lon, 2)
    tokens, depth = xm.shape
    groups, _, width = wbuf.shape[0], wbuf.shape[1], wbuf.shape[2] // 3
    inner = ag.shape[2]
    partner = (lon + 1 - 2 * core, head)
    outer = (lax.rem(lon + 2 * core - 1 + lons, lons), head)
    left, right = (lon - 2, head), (lon + 2, head)

    def other_head(j):
        return lax.rem(head + j, heads)

    def remote(src, dst, send, recv, target):
        return pltpu.make_async_remote_copy(
            src_ref=src, dst_ref=dst, send_sem=send, recv_sem=recv,
            device_id=target, device_id_type=MESH,
        )

    barrier = pltpu.get_barrier_semaphore()
    peers = [outer]
    for dz in range(1, line):
        peers.append((2 * lax.rem(z + dz, line) + core, head))
    for j in range(heads):
        if j:
            peers.append((lon, other_head(j)))
        peers.append((partner[0], other_head(j)))
    for target in peers:
        pl.semaphore_signal(barrier, inc=1, device_id=target, device_id_type=MESH)
    pl.semaphore_wait(barrier, len(peers))

    def chunk(stream, s):
        if isinstance(stream, str) and stream == "text":
            rows = text_hbm.shape[1]
            at = pl.ds(pl.multiple_of(s * rows, rows), rows)
            return text_hbm, tbuf.at[:, at, :], sem_t_s, sem_t_r.at[s]
        if isinstance(stream, str):
            rows = proj_hbm.shape[0]
            at = pl.ds(pl.multiple_of(s * rows, rows), rows)
            return proj_hbm, pbuf.at[at, :], sem_p_s, sem_p_r.at[s]
        rows = w_hbm.shape[1]
        at = pl.ds(pl.multiple_of(s * rows, rows), rows)
        return w_hbm.at[stream], wbuf.at[stream, at, :], sem_w_s.at[stream], sem_w_r.at[stream, s]

    def own_copies(stream):
        src, dst, send, recv = chunk(stream, lon)
        return (
            pltpu.make_async_copy(src, dst, recv),
            remote(src, dst, send.at[0, z], recv, left),
            remote(src, dst, send.at[1, z], recv, right),
            remote(src, dst, send.at[2, z], recv, partner),
        )

    def start_own(stream):
        here, to_left, to_right, to_partner = own_copies(stream)

        @pl.when(z > 0)
        def _():
            to_left.start()

        @pl.when(z < line - 1)
        def _():
            to_right.start()

        to_partner.start()
        here.start()

    def arrived(stream, s):
        _, dst, send, recv = chunk(stream, s)
        return remote(dst, dst, send.at[2, z], recv, partner)

    def forward(stream, d):
        @pl.when(z + d < line)
        def _():
            zz = z + d
            arrived(stream, 2 * zz + core).wait_recv()
            _, dst, send, recv = chunk(stream, 2 * zz + core)

            @pl.when(z > 0)
            def _():
                remote(dst, dst, send.at[0, zz], recv, left).start()

            remote(dst, dst, send.at[2, zz], recv, partner).start()

        @pl.when(z - d >= 0)
        def _():
            zz = z - d
            arrived(stream, 2 * zz + core).wait_recv()
            _, dst, send, recv = chunk(stream, 2 * zz + core)

            @pl.when(z < line - 1)
            def _():
                remote(dst, dst, send.at[1, zz], recv, right).start()

            remote(dst, dst, send.at[2, zz], recv, partner).start()

    def wait_all(stream):
        own_copies(stream)[0].wait()
        for zz in range(line):
            arrived(stream, 2 * zz + 1 - core).wait_recv()

    def wait_sends(stream):
        for zz in range(line):
            _, dst, send, recv = chunk(stream, 2 * zz + core)

            @pl.when((z > 0) & (zz >= z))
            def _():
                remote(dst, dst, send.at[0, zz], recv, left).wait_send()

            @pl.when((z < line - 1) & (zz <= z))
            def _():
                remote(dst, dst, send.at[1, zz], recv, right).wait_send()

            remote(dst, dst, send.at[2, zz], recv, partner).wait_send()

    slot = core * heads + head

    def plane_copies():
        copies = []
        for k in range(2):
            for j in range(heads):
                if k == 0 and j == 0:
                    continue
                target = (lon if k == 0 else partner[0], other_head(j))
                n = k * heads + j
                copies.append(remote(part_ref, pa.at[slot], sem_pa_s.at[n], sem_pa_r.at[slot], target))
        return copies

    def line_copies():
        return [
            remote(
                mod, pb.at[z], sem_pb_s.at[dz], sem_pb_r.at[z],
                (2 * lax.rem(z + dz, line) + core, head),
            )
            for dz in range(1, line)
        ]

    start_own(0)
    x_tile = min(128, tokens)
    x_tiles = tokens // x_tile

    def x_copy(i):
        at = pl.ds(pl.multiple_of(i * x_tile, x_tile), x_tile)
        return pltpu.make_async_copy(x_hbm.at[at, :], xm.at[at, :], sem_x.at[i])

    for i in range(x_tiles):
        x_copy(i).start()
    out_cols = img.shape[1]
    col = pl.multiple_of(head * out_cols, out_cols)
    img_copy = pltpu.make_async_copy(x_hbm.at[:, pl.ds(col, out_cols)], img, sem_img)
    img_copy.start()

    for copy in plane_copies():
        copy.start()
    pa[slot] = part_ref[...]

    block = QROWS * cols
    row_blocks = tokens // block
    side_of_outer = 2 * core - 1
    query = lax.broadcasted_iota(jnp.int32, (block, 3 * block), 0)
    key = lax.broadcasted_iota(jnp.int32, (block, 3 * block), 1)
    row_gap = key // cols - QROWS - query // cols
    for n, side in enumerate((side_of_outer, 0, -side_of_outer)):
        col_gap = key % cols + side * cols - query % cols
        inside = (jnp.abs(row_gap) <= RADIUS) & (jnp.abs(col_gap) <= RADIUS)
        near[n] = jnp.where(inside, 0.0, -1e30).astype(near.dtype)

    for k in range(2):
        for j in range(heads):
            if k == 0 and j == 0:
                continue
            there = (core if k == 0 else 1 - core) * heads + other_head(j)
            remote(part_ref, pa.at[there], sem_pa_s.at[0], sem_pa_r.at[there], outer).wait_recv()
    total = pa[0]
    for n in range(1, 2 * heads):
        total = total + pa[n]
    mod[...] = total
    pb[z] = total
    for copy in line_copies():
        copy.start()
    start_own("text")
    for dz in range(1, line):
        zz = lax.rem(z + dz, line)
        remote(mod, pb.at[zz], sem_pb_s.at[0], sem_pb_r.at[zz], outer).wait_recv()
    for copy in line_copies():
        copy.wait_send()
    total = mod_bias_ref[...]
    for n in range(line):
        total = total + pb[n]
    mod[...] = total

    step_rows = min(32, x_tile)

    def norm_tile(i):
        x_copy(i).wait()

        def one(j, carry):
            at = pl.ds(pl.multiple_of(i * x_tile + j * step_rows, step_rows), step_rows)
            v = xm[at, :].astype(jnp.float32)
            centred = v - jnp.mean(v, axis=1, keepdims=True)
            variance = jnp.mean(centred * centred, axis=1, keepdims=True)
            scaled = (1.0 + mod[1:2, :]) * (centred * lax.rsqrt(variance + 1e-06)) + mod[0:1, :]
            xm[at, :] = scaled.astype(xm.dtype)
            return carry

        lax.fori_loop(0, x_tile // step_rows, one, 0)

    share = tokens // heads

    def share_at(h):
        return pl.ds(pl.multiple_of(h * share, share), share)

    def halo_copy():
        return remote(xm.at[share_at(head), :], xh.at[share_at(head), :], sem_h_s, sem_h_r, outer)

    def spread_copies():
        return [
            remote(
                xh.at[share_at(head), :], xh.at[share_at(head), :],
                sem_f_s.at[j], sem_f_r.at[head], (lon, other_head(j)),
            )
            for j in range(1, heads)
        ]

    def spread():
        halo_copy().wait_recv()
        for copy in spread_copies():
            copy.start()

    def wait_halo():
        for j in range(1, heads):
            h = other_head(j)
            remote(
                xh.at[share_at(h), :], xh.at[share_at(h), :], sem_f_s.at[0], sem_f_r.at[h], outer
            ).wait_recv()

    tile = min(256, tokens)

    def normed(raw, gain_ref):
        pieces = []
        for h in range(width // head_dim):
            entries = raw[:, h * head_dim : (h + 1) * head_dim]
            mean_square = jnp.mean(entries * entries, axis=-1, keepdims=True)
            pieces.append((entries * lax.rsqrt(mean_square + 1e-06) * gain_ref[...]).astype(jnp.bfloat16))
        return pieces

    def product(x_ref, at, g, which):
        cols_at = slice(which * width, (which + 1) * width)
        raw = jnp.dot(x_ref[at, :], wbuf[g, :, cols_at], preferred_element_type=jnp.float32)
        return raw + qkv_bias_ref[g, :, cols_at]

    def put(dst, at, pieces):
        for h, piece in enumerate(pieces):
            dst[at, h * head_dim : (h + 1) * head_dim] = piece

    def project_own(g, i):
        at = pl.ds(pl.multiple_of(i * tile, tile), tile)
        put(kv_own.at[g, 0], at, normed(product(xm, at, g, 0), k_gain_ref))
        kv_own[g, 1, at, :] = product(xm, at, g, 1).astype(jnp.bfloat16)
        put(q_buf, at, normed(product(xm, at, g, 2), q_gain_ref))

    def project_halo(g, i):
        at = pl.ds(pl.multiple_of(i * tile, tile), tile)
        put(kv_outer.at[0], at, normed(product(xh, at, g, 0), k_gain_ref))
        kv_outer[1, at, :] = product(xh, at, g, 1).astype(jnp.bfloat16)

    def kv_copy(g):
        return remote(kv_own.at[g], kv_inner.at[g], sem_kv_s.at[g], sem_kv_r.at[g], partner)

    factor = math.log2(math.e) / math.sqrt(head_dim)
    contract = (((1,), (1,)), ((), ()))

    def attend(g, qb):
        low, high = max(qb - 1, 0), min(qb + 2, row_blocks)
        first = (low - qb + 1) * block
        span = (high - low) * block
        rows_q = slice(qb * block, (qb + 1) * block)
        rows_k = slice(low * block, high * block)

        def one_head(hh, carry):
            lanes = pl.ds(pl.multiple_of(hh * head_dim, head_dim), head_dim)
            text_lanes = pl.ds(pl.multiple_of(g * width + hh * head_dim, head_dim), head_dim)
            q = q_buf[rows_q, lanes]
            scores = []
            values = []
            for n, kv in enumerate((kv_outer, kv_own.at[g], kv_inner.at[g])):
                s = lax.dot_general(q, kv[0, rows_k, lanes], contract, preferred_element_type=jnp.float32)
                scores.append(s + near[n, :, first : first + span])
                values.append(kv[1, rows_k, lanes])
            scores.append(
                lax.dot_general(q, tbuf[0, :, text_lanes], contract, preferred_element_type=jnp.float32)
            )
            values.append(tbuf[1, :, text_lanes])
            highest = functools.reduce(
                jnp.maximum, [jnp.max(s, axis=1, keepdims=True) for s in scores]
            )
            total = 0.0
            out = 0.0
            for s, v in zip(scores, values):
                p = jnp.exp2((s - highest) * factor)
                total = total + jnp.sum(p, axis=1, keepdims=True)
                out = out + jnp.dot(p.astype(jnp.bfloat16), v, preferred_element_type=jnp.float32)
            ag[head, rows_q, text_lanes] = (out / total).astype(ag.dtype)
            return carry

        lax.fori_loop(0, width // head_dim, one_head, 0)

    def share_copies(g, qb):
        piece = ag.at[head, pl.ds(qb * block, block), pl.ds(pl.multiple_of(g * width, width), width)]
        n = g * row_blocks + qb
        return [
            remote(piece, piece, sem_a_s.at[j, n], sem_a_r.at[head, n], (lon, other_head(j)))
            for j in range(1, heads)
        ]

    def wait_shares(g, qb):
        n = g * row_blocks + qb
        for j in range(1, heads):
            h = other_head(j)
            piece = ag.at[h, pl.ds(qb * block, block), pl.ds(pl.multiple_of(g * width, width), width)]
            remote(piece, piece, sem_a_s.at[0, n], sem_a_r.at[h, n], outer).wait_recv()

    tiles = tokens // tile

    def start_stream(n):
        @pl.when(n < groups)
        def _():
            start_own(n)

        @pl.when(n == groups)
        def _():
            start_own("proj")

    def forward_stream(n, d):
        @pl.when(n < groups)
        def _():
            forward(n, d)

        @pl.when(n == groups)
        def _():
            forward("proj", d)

    forward(0, 1)

    def norm_step(i, carry):
        norm_tile(i)
        if line > 2:

            @pl.when(i == x_tiles // 2)
            def _():
                forward(0, 2)

        return carry

    lax.fori_loop(0, x_tiles, norm_step, 0)
    halo_copy().start()
    start_own(1)
    for d in range(3, line):
        forward(0, d)
    for d in range(1, line):
        forward("text", d)

    def group_step(g, carry):
        wait_all(g)

        def own_step(i, carry):
            project_own(g, i)

            @pl.when(i == 0)
            def _():
                forward_stream(g + 1, 1)

            return carry

        lax.fori_loop(0, tiles, own_step, 0)
        kv_copy(g).start()

        @pl.when(g == 0)
        def _():
            spread()

        start_stream(g + 2)
        if line > 2:
            forward_stream(g + 1, 2)

        @pl.when(g == 0)
        def _():
            wait_halo()

        def halo_step(i, carry):
            project_halo(g, i)

            if line > 3:

                @pl.when(i == 1)
                def _():
                    forward_stream(g + 1, 3)

            return carry

        lax.fori_loop(0, tiles, halo_step, 0)
        for d in range(4, line):
            forward_stream(g + 1, d)

        @pl.when(g == 0)
        def _():
            wait_all("text")

        kv_copy(g).wait_recv()
        for qb in range(row_blocks):
            attend(g, qb)
            for copy in share_copies(g, qb):
                copy.start()
        return carry

    lax.fori_loop(0, groups, group_step, 0)

    wait_all("proj")
    img_copy.wait()
    gate = mod[2:3, pl.ds(col, out_cols)]

    def out_copy(qb):
        at = pl.ds(pl.multiple_of(qb * block, block), block)
        return pltpu.make_async_copy(img.at[at, :], out_hbm.at[at, :], sem_out.at[qb])

    def out_step(qb, carry):
        for g in range(groups):
            wait_shares(g, qb)
        rows = pl.ds(pl.multiple_of(qb * block, block), block)
        total = proj_bias_ref[...]
        for k in range(heads):
            total = total + jnp.dot(
                ag[k, rows, :], pbuf[k * inner : (k + 1) * inner, :], preferred_element_type=jnp.float32
            )
        img[rows, :] = (img[rows, :].astype(jnp.float32) + gate * total).astype(img.dtype)
        out_copy(qb).start()
        return carry

    lax.fori_loop(0, row_blocks, out_step, 0)

    for copy in plane_copies():
        copy.wait_send()
    wait_sends("text")
    wait_sends("proj")

    def sent_step(g, carry):
        wait_sends(g)
        kv_copy(g).wait_send()
        for qb in range(row_blocks):
            for copy in share_copies(g, qb):
                copy.wait_send()
        return carry

    lax.fori_loop(0, groups, sent_step, 0)
    halo_copy().wait_send()
    for copy in spread_copies():
        copy.wait_send()
    for qb in range(row_blocks):
        out_copy(qb).wait()


def body(
    image_tokens,
    conditioning,
    mod_weight,
    mod_bias,
    qkv_weight,
    qkv_bias,
    q_gain,
    k_gain,
    text_kv,
    proj_weight,
    proj_bias,
):
    lat_rows, cols, depth = image_tokens.shape
    tokens = lat_rows * cols
    lons, heads = lax.axis_size("lon"), lax.axis_size("head")
    line = lons // 2
    rows, _, inner = qkv_weight.shape
    head_dim = q_gain.shape[0]
    groups = 3
    width = inner // groups
    text_rows = text_kv.shape[1]
    out_cols = proj_weight.shape[1]
    block = QROWS * cols
    row_blocks = tokens // block

    w = qkv_weight.reshape(rows, 3, groups, width).transpose(2, 0, 1, 3)
    w = jnp.concatenate([w[:, :, 1:], w[:, :, :1]], axis=2).reshape(groups, rows, 3 * width)
    b = qkv_bias.astype(jnp.float32).reshape(3, groups, width).transpose(1, 0, 2)
    b = jnp.concatenate([b[:, 1:], b[:, :1]], axis=1).reshape(groups, 1, 3 * width)

    slice_rows = mod_weight.shape[0]
    first = (lax.axis_index("lon") * heads + lax.axis_index("head")) * slice_rows
    silu_part = jax.nn.silu(
        lax.dynamic_slice_in_dim(conditioning, first, slice_rows, 0).astype(jnp.float32)
    )
    part = jnp.dot(
        silu_part,
        mod_weight.reshape(slice_rows, 3 * depth).astype(jnp.float32),
        precision=lax.Precision.HIGHEST,
    ).reshape(3, depth)
    own_bias = lax.dynamic_slice_in_dim(
        proj_bias, lax.axis_index("head") * out_cols, out_cols, 0
    ).astype(jnp.float32)

    x_tiles = tokens // min(128, tokens)
    vmem = pl.BlockSpec(memory_space=pltpu.VMEM)
    anywhere = pl.BlockSpec(memory_space=pl.ANY)
    dma = pltpu.SemaphoreType.DMA
    out = pl.pallas_call(
        functools.partial(kernel, (lons, heads, cols, head_dim)),
        out_shape=jax.ShapeDtypeStruct((tokens, out_cols), jnp.bfloat16),
        in_specs=[anywhere, vmem, vmem, anywhere, vmem, vmem, vmem, anywhere, anywhere, vmem],
        out_specs=anywhere,
        scratch_shapes=[
            pltpu.VMEM((tokens, depth), jnp.bfloat16),
            pltpu.VMEM((tokens, depth), jnp.bfloat16),
            pltpu.VMEM((groups, depth, 3 * width), jnp.bfloat16),
            pltpu.VMEM((heads * inner, out_cols), jnp.bfloat16),
            pltpu.VMEM((2, lons * text_rows, inner), jnp.bfloat16),
            pltpu.VMEM((groups, 2, tokens, width), jnp.bfloat16),
            pltpu.VMEM((groups, 2, tokens, width), jnp.bfloat16),
            pltpu.VMEM((2, tokens, width), jnp.bfloat16),
            pltpu.VMEM((tokens, width), jnp.bfloat16),
            pltpu.VMEM((heads, tokens, inner), jnp.bfloat16),
            pltpu.VMEM((tokens, out_cols), jnp.bfloat16),
            pltpu.VMEM((3, block, 3 * block), jnp.float32),
            pltpu.VMEM((2 * heads, 3, depth), jnp.float32),
            pltpu.VMEM((line, 3, depth), jnp.float32),
            pltpu.VMEM((3, depth), jnp.float32),
            dma((2 * heads,)),
            dma((2 * heads,)),
            dma((line,)),
            dma((line,)),
            dma((groups, 3, line)),
            dma((groups, lons)),
            dma((3, line)),
            dma((lons,)),
            dma((3, line)),
            dma((lons,)),
            dma,
            dma,
            dma((heads,)),
            dma((heads,)),
            dma((groups,)),
            dma((groups,)),
            dma((heads, groups * row_blocks)),
            dma((heads, groups * row_blocks)),
            dma((x_tiles,)),
            dma,
            dma((row_blocks,)),
        ],
        compiler_params=pltpu.CompilerParams(
            collective_id=0, has_side_effects=True, vmem_limit_bytes=VMEM_LIMIT
        ),
        cost_estimate=pl.CostEstimate(
            flops=2 * tokens * depth * inner * 6, bytes_accessed=8 * tokens * depth, transcendentals=0
        ),
    )(
        image_tokens.reshape(tokens, depth),
        part,
        mod_bias.astype(jnp.float32),
        w,
        b,
        q_gain.reshape(1, head_dim),
        k_gain.reshape(1, head_dim),
        text_kv,
        proj_weight,
        own_bias.reshape(1, out_cols),
    )
    return out.reshape(lat_rows, cols, out_cols)


def solution(mesh):
    placed = (
        P(None, "lon", None),
        P(),
        P(("lon", "head"), None, None),
        P(),
        P("lon", None, "head"),
        P(None, "head"),
        P(),
        P(),
        P(None, "lon", "head"),
        P("lon", "head"),
        P(),
    )
    return jax.shard_map(
        body, mesh=mesh, in_specs=placed, out_specs=P(None, "lon", "head"), check_vma=False
    )
```

```python
import functools
import math

import jax
import jax.numpy as jnp
from jax import lax
from jax.experimental import pallas as pl
from jax.experimental.pallas import tpu as pltpu
from jax.sharding import PartitionSpec as P

RADIUS = 15
QROWS = 16
VMEM_LIMIT = 63 * 1024 * 1024
MESH = pl.DeviceIdType.MESH


def kernel(
    sizes,
    x_hbm,
    part_ref,
    mod_bias_ref,
    w_hbm,
    qkv_bias_ref,
    q_gain_ref,
    k_gain_ref,
    text_hbm,
    proj_hbm,
    proj_bias_ref,
    out_hbm,
    xm,
    xh,
    wbuf,
    pbuf,
    tbuf,
    kv_own,
    kv_inner,
    kv_outer,
    q_buf,
    ag,
    img,
    near,
    pa,
    pb,
    mod,
    sem_pa_s,
    sem_pa_r,
    sem_pb_s,
    sem_pb_r,
    sem_w_s,
    sem_w_r,
    sem_p_s,
    sem_p_r,
    sem_t_s,
    sem_t_r,
    sem_h_s,
    sem_h_r,
    sem_f_s,
    sem_f_r,
    sem_kv_s,
    sem_kv_r,
    sem_a_s,
    sem_a_r,
    sem_x,
    sem_img,
    sem_out,
):
    lons, heads, cols, head_dim = sizes
    line = lons // 2
    lon, head = lax.axis_index("lon"), lax.axis_index("head")
    z, core = lon // 2, lax.rem(lon, 2)
    tokens, depth = xm.shape
    groups, width = wbuf.shape[0], wbuf.shape[3]
    inner = ag.shape[2]
    partner = (lon + 1 - 2 * core, head)
    outer = (lax.rem(lon + 2 * core - 1 + lons, lons), head)
    left, right = (lon - 2, head), (lon + 2, head)

    def other_head(j):
        return lax.rem(head + j, heads)

    def remote(src, dst, send, recv, target):
        return pltpu.make_async_remote_copy(
            src_ref=src, dst_ref=dst, send_sem=send, recv_sem=recv,
            device_id=target, device_id_type=MESH,
        )

    barrier = pltpu.get_barrier_semaphore()
    peers = [outer]
    for dz in range(1, line):
        peers.append((2 * lax.rem(z + dz, line) + core, head))
    for j in range(heads):
        if j:
            peers.append((lon, other_head(j)))
        peers.append((partner[0], other_head(j)))
    for target in peers:
        pl.semaphore_signal(barrier, inc=1, device_id=target, device_id_type=MESH)
    pl.semaphore_wait(barrier, len(peers))

    def chunk(stream, s):
        if isinstance(stream, str) and stream == "text":
            rows = text_hbm.shape[1]
            at = pl.ds(pl.multiple_of(s * rows, rows), rows)
            return text_hbm, tbuf.at[:, at, :], sem_t_s, sem_t_r.at[s]
        if isinstance(stream, str):
            rows = proj_hbm.shape[0]
            at = pl.ds(pl.multiple_of(s * rows, rows), rows)
            return proj_hbm, pbuf.at[at, :], sem_p_s, sem_p_r.at[s]
        rows = w_hbm.shape[1]
        at = pl.ds(pl.multiple_of(s * rows, rows), rows)
        part = pl.ds(pl.multiple_of(stream * width, width), width)
        return w_hbm.at[:, :, part], wbuf.at[stream, :, at, :], sem_w_s.at[stream], sem_w_r.at[stream, s]

    def own_copies(stream):
        src, dst, send, recv = chunk(stream, lon)
        return (
            pltpu.make_async_copy(src, dst, recv),
            remote(src, dst, send.at[0, z], recv, left),
            remote(src, dst, send.at[1, z], recv, right),
            remote(src, dst, send.at[2, z], recv, partner),
        )

    def start_own(stream):
        here, to_left, to_right, to_partner = own_copies(stream)

        @pl.when(z > 0)
        def _():
            to_left.start()

        @pl.when(z < line - 1)
        def _():
            to_right.start()

        to_partner.start()
        here.start()

    def arrived(stream, s):
        _, dst, send, recv = chunk(stream, s)
        return remote(dst, dst, send.at[2, z], recv, partner)

    def pass_on(stream, zz, way, target, more):
        arrived(stream, 2 * zz + core).wait_recv()
        _, dst, send, recv = chunk(stream, 2 * zz + core)

        @pl.when(more)
        def _():
            remote(dst, dst, send.at[way, zz], recv, target).start()

        remote(dst, dst, send.at[2, zz], recv, partner).start()

    def forward(stream, d):
        @pl.when(z + d < line)
        def _():
            pass_on(stream, z + d, 0, left, z > 0)

        @pl.when(z - d >= 0)
        def _():
            pass_on(stream, z - d, 1, right, z < line - 1)

    at_end = (z == 0) | (z == line - 1)

    def relay(*steps):
        @pl.when(jnp.logical_not(at_end))
        def _():
            for stream, d in steps:
                forward(stream, d)

    def take(stream):
        @pl.when(at_end)
        def _():
            for d in range(1, line):
                forward(stream, d)

        wait_all(stream)

    def wait_all(stream):
        own_copies(stream)[0].wait()
        for zz in range(line):
            arrived(stream, 2 * zz + 1 - core).wait_recv()

    def wait_sends(stream):
        for zz in range(line):
            _, dst, send, recv = chunk(stream, 2 * zz + core)

            @pl.when((z > 0) & (zz >= z))
            def _():
                remote(dst, dst, send.at[0, zz], recv, left).wait_send()

            @pl.when((z < line - 1) & (zz <= z))
            def _():
                remote(dst, dst, send.at[1, zz], recv, right).wait_send()

            remote(dst, dst, send.at[2, zz], recv, partner).wait_send()

    slot = core * heads + head

    def plane_copies():
        copies = []
        for k in range(2):
            for j in range(heads):
                if k == 0 and j == 0:
                    continue
                target = (lon if k == 0 else partner[0], other_head(j))
                n = k * heads + j
                copies.append(remote(part_ref, pa.at[slot], sem_pa_s.at[n], sem_pa_r.at[slot], target))
        return copies

    def line_copies():
        return [
            remote(
                mod, pb.at[z], sem_pb_s.at[dz], sem_pb_r.at[z],
                (2 * lax.rem(z + dz, line) + core, head),
            )
            for dz in range(1, line)
        ]

    for copy in plane_copies():
        copy.start()
    start_own(0)
    x_tile = min(128, tokens)
    x_tiles = tokens // x_tile

    def x_copy(i):
        at = pl.ds(pl.multiple_of(i * x_tile, x_tile), x_tile)
        return pltpu.make_async_copy(x_hbm.at[at, :], xm.at[at, :], sem_x.at[i])

    for i in range(x_tiles):
        x_copy(i).start()
    out_cols = img.shape[1]
    col = pl.multiple_of(head * out_cols, out_cols)
    img_copy = pltpu.make_async_copy(x_hbm.at[:, pl.ds(col, out_cols)], img, sem_img)
    img_copy.start()

    pa[slot] = part_ref[...]

    for k in range(2):
        for j in range(heads):
            if k == 0 and j == 0:
                continue
            there = (core if k == 0 else 1 - core) * heads + other_head(j)
            remote(part_ref, pa.at[there], sem_pa_s.at[0], sem_pa_r.at[there], outer).wait_recv()
    total = pa[0]
    for n in range(1, 2 * heads):
        total = total + pa[n]
    mod[...] = total
    pb[z] = total
    for copy in line_copies():
        copy.start()
    start_own("text")

    block = QROWS * cols
    row_blocks = tokens // block
    side_of_outer = 2 * core - 1
    query = lax.broadcasted_iota(jnp.int32, (block, 3 * block), 0)
    key = lax.broadcasted_iota(jnp.int32, (block, 3 * block), 1)
    row_gap = key // cols - QROWS - query // cols
    for n, side in enumerate((side_of_outer, 0, -side_of_outer)):
        col_gap = key % cols + side * cols - query % cols
        inside = (jnp.abs(row_gap) <= RADIUS) & (jnp.abs(col_gap) <= RADIUS)
        near[n] = jnp.where(inside, 0.0, -1e30).astype(near.dtype)

    for dz in range(1, line):
        zz = lax.rem(z + dz, line)
        remote(mod, pb.at[zz], sem_pb_s.at[0], sem_pb_r.at[zz], outer).wait_recv()
    for copy in line_copies():
        copy.wait_send()
    total = mod_bias_ref[...].astype(jnp.float32)
    for n in range(line):
        total = total + pb[n]
    mod[...] = total

    step_rows = min(32, x_tile)

    def norm_tile(i):
        x_copy(i).wait()

        def one(j, carry):
            at = pl.ds(pl.multiple_of(i * x_tile + j * step_rows, step_rows), step_rows)
            v = xm[at, :].astype(jnp.float32)
            centred = v - jnp.mean(v, axis=1, keepdims=True)
            variance = jnp.mean(centred * centred, axis=1, keepdims=True)
            scaled = (1.0 + mod[1:2, :]) * (centred * lax.rsqrt(variance + 1e-06)) + mod[0:1, :]
            xm[at, :] = scaled.astype(xm.dtype)
            return carry

        lax.fori_loop(0, x_tile // step_rows, one, 0)

    share = tokens // heads

    def share_at(h):
        return pl.ds(pl.multiple_of(h * share, share), share)

    def halo_copy():
        return remote(xm.at[share_at(head), :], xh.at[share_at(head), :], sem_h_s, sem_h_r, outer)

    x_peer, y_peer = head + 1 - 2 * lax.rem(head, 2), head + 2 - 4 * (head // 2)
    half = share // 2

    def spread_copy(part, h, n, target):
        at = pl.ds(pl.multiple_of(h * share + part * half, half), half)
        return remote(
            xh.at[at, :], xh.at[at, :], sem_f_s.at[part, n], sem_f_r.at[part, h], (lon, target)
        )

    def spread_first():
        if heads != 4:
            return [
                spread_copy(part, head, j, other_head(j)) for part in range(2) for j in range(1, heads)
            ]
        return [
            spread_copy(0, head, 1, x_peer),
            spread_copy(1, head, 1, y_peer),
            spread_copy(0, head, 2, y_peer),
            spread_copy(1, head, 2, x_peer),
        ]

    def spread_second():
        if heads != 4:
            return []
        return [spread_copy(0, x_peer, 3, y_peer), spread_copy(1, y_peer, 3, x_peer)]

    def spread():
        halo_copy().wait_recv()
        for copy in spread_first():
            copy.start()

    def spread_on():
        if heads == 4:
            spread_copy(0, x_peer, 0, x_peer).wait_recv()
            spread_copy(1, y_peer, 0, x_peer).wait_recv()
            for copy in spread_second():
                copy.start()

    def wait_halo():
        for j in range(1, heads):
            h = other_head(j)
            for part in range(2):
                if heads == 4:

                    @pl.when(h != (x_peer, y_peer)[part])
                    def _():
                        spread_copy(part, h, 0, x_peer).wait_recv()

                else:
                    spread_copy(part, h, 0, head).wait_recv()

    tile = min(256, tokens)

    def normed(raw, gain_ref):
        pieces = []
        for h in range(width // head_dim):
            entries = raw[:, h * head_dim : (h + 1) * head_dim]
            mean_square = jnp.mean(entries * entries, axis=-1, keepdims=True)
            pieces.append((entries * lax.rsqrt(mean_square + 1e-06) * gain_ref[...]).astype(jnp.bfloat16))
        return pieces

    def product(x_ref, at, g, which):
        raw = jnp.dot(x_ref[at, :], wbuf[g, which], preferred_element_type=jnp.float32)
        part = pl.ds(pl.multiple_of(g * width, width), width)
        return raw + qkv_bias_ref[which : which + 1, part].astype(jnp.float32)

    def put(dst, at, pieces):
        for h, piece in enumerate(pieces):
            dst[at, h * head_dim : (h + 1) * head_dim] = piece

    def project_own(g, i):
        at = pl.ds(pl.multiple_of(i * tile, tile), tile)
        put(kv_own.at[g, 0], at, normed(product(xm, at, g, 1), k_gain_ref))
        kv_own[g, 1, at, :] = product(xm, at, g, 2).astype(jnp.bfloat16)
        put(q_buf, at, normed(product(xm, at, g, 0), q_gain_ref))

    def project_halo(g, i):
        at = pl.ds(pl.multiple_of(i * tile, tile), tile)
        put(kv_outer.at[0], at, normed(product(xh, at, g, 1), k_gain_ref))
        kv_outer[1, at, :] = product(xh, at, g, 2).astype(jnp.bfloat16)

    def kv_copy(g):
        return remote(kv_own.at[g], kv_inner.at[g], sem_kv_s.at[g], sem_kv_r.at[g], partner)

    factor = math.log2(math.e) / math.sqrt(head_dim)
    contract = (((1,), (1,)), ((), ()))

    def attend(g, qb):
        low, high = max(qb - 1, 0), min(qb + 2, row_blocks)
        first = (low - qb + 1) * block
        span = (high - low) * block
        rows_q = slice(qb * block, (qb + 1) * block)
        rows_k = slice(low * block, high * block)

        def one_head(hh, carry):
            lanes = pl.ds(pl.multiple_of(hh * head_dim, head_dim), head_dim)
            text_lanes = pl.ds(pl.multiple_of(g * width + hh * head_dim, head_dim), head_dim)
            q = q_buf[rows_q, lanes]
            scores = []
            values = []
            for n, kv in enumerate((kv_outer, kv_own.at[g], kv_inner.at[g])):
                s = lax.dot_general(q, kv[0, rows_k, lanes], contract, preferred_element_type=jnp.float32)
                scores.append(s + near[n, :, first : first + span])
                values.append(kv[1, rows_k, lanes])
            scores.append(
                lax.dot_general(q, tbuf[0, :, text_lanes], contract, preferred_element_type=jnp.float32)
            )
            values.append(tbuf[1, :, text_lanes])
            highest = functools.reduce(
                jnp.maximum, [jnp.max(s, axis=1, keepdims=True) for s in scores]
            )
            total = 0.0
            out = 0.0
            for s, v in zip(scores, values):
                p = jnp.exp2((s - highest) * factor)
                total = total + jnp.sum(p, axis=1, keepdims=True)
                out = out + jnp.dot(p.astype(jnp.bfloat16), v, preferred_element_type=jnp.float32)
            ag[head, rows_q, text_lanes] = (out / total).astype(ag.dtype)
            return carry

        lax.fori_loop(0, width // head_dim, one_head, 0)

    far = heads - 1 - head

    def share_copy(h, g, qb, part, recv, send, target):
        rows = block if part is None else block // 2
        first = qb * block + (0 if part is None else part * rows)
        piece = ag.at[
            h, pl.ds(pl.multiple_of(first, rows), rows), pl.ds(pl.multiple_of(g * width, width), width)
        ]
        n = g * row_blocks + qb
        return remote(piece, piece, sem_a_s.at[send, n], sem_a_r.at[recv, n], (lon, target))

    def share_copies(g, qb):
        if heads != 4:
            return [
                share_copy(head, g, qb, None, head, j, other_head(j)) for j in range(1, heads)
            ]
        return [
            share_copy(head, g, qb, None, head, 0, x_peer),
            share_copy(head, g, qb, None, head, 1, y_peer),
        ]

    def passed_copies(g, qb):
        if heads != 4:
            return []
        return [
            share_copy(x_peer, g, qb, 0, x_peer, 2, y_peer),
            share_copy(y_peer, g, qb, 1, heads, 3, x_peer),
        ]

    def pass_shares(g, qb):
        if heads == 4:
            for h in (x_peer, y_peer):
                share_copy(h, g, qb, None, h, 0, x_peer).wait_recv()
            for copy in passed_copies(g, qb):
                copy.start()

    def wait_shares(g, qb):
        if heads == 4:
            share_copy(far, g, qb, 0, far, 0, x_peer).wait_recv()
            share_copy(far, g, qb, 1, heads, 0, x_peer).wait_recv()
        else:
            for j in range(1, heads):
                share_copy(other_head(j), g, qb, None, other_head(j), 0, head).wait_recv()

    tiles = tokens // tile
    lag = 2

    def norm_step(i, carry):
        norm_tile(i)
        return carry

    relay((0, 1))
    lax.fori_loop(0, x_tiles, norm_step, 0)
    halo_copy().start()
    relay(("text", 1))
    relay(*[(stream, d) for d in range(2, line) for stream in (0, "text")])
    start_own(1)
    relay((1, 1))
    start_own(2)

    @pl.when(at_end)
    def _():
        start_own("proj")

    spread()
    take(0)

    def group_step(g, carry):
        @pl.when(g > 0)
        def _():
            take(g)

        def own_step(i, carry):
            project_own(g, i)

            for late in range(lag):

                @pl.when((g > 0) & (i == late * tiles // lag))
                def _():
                    pass_shares(g - 1, row_blocks - lag + late)

            @pl.when((g == 1) & (i == 1))
            def _():
                relay(("proj", 1))

            @pl.when((g == 2) & (i == 1))
            def _():
                relay(*[("proj", d) for d in range(2, line)])

            return carry

        lax.fori_loop(0, tiles, own_step, 0)
        kv_copy(g).start()

        @pl.when(g == 0)
        def _():
            spread_on()
            relay(*[(1, d) for d in range(2, line)])
            relay((2, 1))
            wait_halo()

        def halo_step(i, carry):
            project_halo(g, i)
            return carry

        lax.fori_loop(0, tiles, halo_step, 0)

        @pl.when(g == 0)
        def _():
            take("text")

        kv_copy(g).wait_recv()
        for qb in range(row_blocks):
            attend(g, qb)
            for copy in share_copies(g, qb):
                copy.start()
            if qb >= lag:
                pass_shares(g, qb - lag)
            if qb == 1:

                @pl.when((g == 0) & jnp.logical_not(at_end))
                def _():
                    relay(*[(2, d) for d in range(2, line)])
                    start_own("proj")
        return carry

    lax.fori_loop(0, groups, group_step, 0)
    for late in range(lag):
        pass_shares(groups - 1, row_blocks - lag + late)

    take("proj")
    img_copy.wait()
    gate = mod[2:3, pl.ds(col, out_cols)]

    def out_copy(qb):
        at = pl.ds(pl.multiple_of(qb * block, block), block)
        return pltpu.make_async_copy(img.at[at, :], out_hbm.at[at, :], sem_out.at[qb])

    def out_step(qb, carry):
        for g in range(groups):
            wait_shares(g, qb)
        rows = pl.ds(pl.multiple_of(qb * block, block), block)
        total = proj_bias_ref[:, pl.ds(col, out_cols)].astype(jnp.float32)
        for k in range(heads):
            total = total + jnp.dot(
                ag[k, rows, :], pbuf[k * inner : (k + 1) * inner, :], preferred_element_type=jnp.float32
            )
        img[rows, :] = (img[rows, :].astype(jnp.float32) + gate * total).astype(img.dtype)
        out_copy(qb).start()
        return carry

    lax.fori_loop(0, row_blocks, out_step, 0)

    for copy in plane_copies():
        copy.wait_send()
    wait_sends("text")
    wait_sends("proj")

    def sent_step(g, carry):
        wait_sends(g)
        kv_copy(g).wait_send()
        for qb in range(row_blocks):
            for copy in share_copies(g, qb) + passed_copies(g, qb):
                copy.wait_send()
        return carry

    lax.fori_loop(0, groups, sent_step, 0)
    halo_copy().wait_send()
    for copy in spread_first() + spread_second():
        copy.wait_send()
    for qb in range(row_blocks):
        out_copy(qb).wait()


def body(
    image_tokens,
    conditioning,
    mod_weight,
    mod_bias,
    qkv_weight,
    qkv_bias,
    q_gain,
    k_gain,
    text_kv,
    proj_weight,
    proj_bias,
):
    lat_rows, cols, depth = image_tokens.shape
    tokens = lat_rows * cols
    lons, heads = lax.axis_size("lon"), lax.axis_size("head")
    line = lons // 2
    rows, _, inner = qkv_weight.shape
    head_dim = q_gain.shape[0]
    groups = 3
    width = inner // groups
    text_rows = text_kv.shape[1]
    out_cols = proj_weight.shape[1]
    block = QROWS * cols
    row_blocks = tokens // block

    w = qkv_weight.transpose(1, 0, 2)

    slice_rows = mod_weight.shape[0]
    first = (lax.axis_index("lon") * heads + lax.axis_index("head")) * slice_rows
    silu_part = jax.nn.silu(
        lax.dynamic_slice_in_dim(conditioning, first, slice_rows, 0).astype(jnp.float32)
    )
    part = jnp.dot(
        silu_part,
        mod_weight.reshape(slice_rows, 3 * depth).astype(jnp.float32),
        precision=lax.Precision.HIGHEST,
    ).reshape(3, depth)
    x_tiles = tokens // min(128, tokens)
    vmem = pl.BlockSpec(memory_space=pltpu.VMEM)
    anywhere = pl.BlockSpec(memory_space=pl.ANY)
    dma = pltpu.SemaphoreType.DMA
    out = pl.pallas_call(
        functools.partial(kernel, (lons, heads, cols, head_dim)),
        out_shape=jax.ShapeDtypeStruct((tokens, out_cols), jnp.bfloat16),
        in_specs=[anywhere, vmem, vmem, anywhere, vmem, vmem, vmem, anywhere, anywhere, vmem],
        out_specs=anywhere,
        scratch_shapes=[
            pltpu.VMEM((tokens, depth), jnp.bfloat16),
            pltpu.VMEM((tokens, depth), jnp.bfloat16),
            pltpu.VMEM((groups, 3, depth, width), jnp.bfloat16),
            pltpu.VMEM((heads * inner, out_cols), jnp.bfloat16),
            pltpu.VMEM((2, lons * text_rows, inner), jnp.bfloat16),
            pltpu.VMEM((groups, 2, tokens, width), jnp.bfloat16),
            pltpu.VMEM((groups, 2, tokens, width), jnp.bfloat16),
            pltpu.VMEM((2, tokens, width), jnp.bfloat16),
            pltpu.VMEM((tokens, width), jnp.bfloat16),
            pltpu.VMEM((heads, tokens, inner), jnp.bfloat16),
            pltpu.VMEM((tokens, out_cols), jnp.bfloat16),
            pltpu.VMEM((3, block, 3 * block), jnp.float32),
            pltpu.VMEM((2 * heads, 3, depth), jnp.float32),
            pltpu.VMEM((line, 3, depth), jnp.float32),
            pltpu.VMEM((3, depth), jnp.float32),
            dma((2 * heads,)),
            dma((2 * heads,)),
            dma((line,)),
            dma((line,)),
            dma((groups, 3, line)),
            dma((groups, lons)),
            dma((3, line)),
            dma((lons,)),
            dma((3, line)),
            dma((lons,)),
            dma,
            dma,
            dma((2, heads)),
            dma((2, heads)),
            dma((groups,)),
            dma((groups,)),
            dma((heads, groups * row_blocks)),
            dma((heads + 1, groups * row_blocks)),
            dma((x_tiles,)),
            dma,
            dma((row_blocks,)),
        ],
        compiler_params=pltpu.CompilerParams(
            collective_id=0, has_side_effects=True, vmem_limit_bytes=VMEM_LIMIT
        ),
        cost_estimate=pl.CostEstimate(
            flops=2 * tokens * depth * inner * 6, bytes_accessed=8 * tokens * depth, transcendentals=0
        ),
    )(
        image_tokens.reshape(tokens, depth),
        part,
        mod_bias,
        w,
        qkv_bias,
        q_gain.reshape(1, head_dim),
        k_gain.reshape(1, head_dim),
        text_kv,
        proj_weight,
        proj_bias.reshape(1, depth),
    )
    return out.reshape(lat_rows, cols, out_cols)


def solution(mesh):
    placed = (
        P(None, "lon", None),
        P(),
        P(("lon", "head"), None, None),
        P(),
        P("lon", None, "head"),
        P(None, "head"),
        P(),
        P(),
        P(None, "lon", "head"),
        P("lon", "head"),
        P(),
    )
    return jax.shard_map(
        body, mesh=mesh, in_specs=placed, out_specs=P(None, "lon", "head"), check_vma=False
    )
```

```python
import functools
import math

import jax
import jax.numpy as jnp
from jax import lax
from jax.experimental import pallas as pl
from jax.experimental.pallas import tpu as pltpu
from jax.sharding import PartitionSpec as P

RADIUS = 15
QROWS = 16
VMEM_LIMIT = 63 * 1024 * 1024
MESH = pl.DeviceIdType.MESH


def kernel(
    sizes,
    x_hbm,
    part_ref,
    mod_bias_ref,
    w_hbm,
    qkv_bias_ref,
    q_gain_ref,
    k_gain_ref,
    text_hbm,
    proj_hbm,
    proj_bias_ref,
    out_hbm,
    xm,
    xh,
    wbuf,
    pbuf,
    tbuf,
    kv_own,
    kv_inner,
    kv_outer,
    q_buf,
    ag,
    img,
    near,
    pa,
    pb,
    mod,
    bias_row,
    sem_pa_s,
    sem_pa_r,
    sem_pb_s,
    sem_pb_r,
    sem_w_s,
    sem_w_r,
    sem_p_s,
    sem_p_r,
    sem_t_s,
    sem_t_r,
    sem_h_s,
    sem_h_r,
    sem_f_s,
    sem_f_r,
    sem_kv_s,
    sem_kv_r,
    sem_a_s,
    sem_a_r,
    sem_x,
    sem_img,
    sem_out,
):
    lons, heads, cols, head_dim = sizes
    line = lons // 2
    lon, head = lax.axis_index("lon"), lax.axis_index("head")
    z, core = lon // 2, lax.rem(lon, 2)
    tokens, depth = xm.shape
    groups, width = wbuf.shape[0], wbuf.shape[3]
    inner = ag.shape[2]
    partner = (lon + 1 - 2 * core, head)
    outer = (lax.rem(lon + 2 * core - 1 + lons, lons), head)
    left, right = (lon - 2, head), (lon + 2, head)

    def other_head(j):
        return lax.rem(head + j, heads)

    def remote(src, dst, send, recv, target):
        return pltpu.make_async_remote_copy(
            src_ref=src, dst_ref=dst, send_sem=send, recv_sem=recv,
            device_id=target, device_id_type=MESH,
        )

    barrier = pltpu.get_barrier_semaphore()
    peers = [outer]
    for dz in range(1, line):
        peers.append((2 * lax.rem(z + dz, line) + core, head))
    for j in range(heads):
        if j:
            peers.append((lon, other_head(j)))
        peers.append((partner[0], other_head(j)))
    for target in peers:
        pl.semaphore_signal(barrier, inc=1, device_id=target, device_id_type=MESH)
    pl.semaphore_wait(barrier, len(peers))

    def chunk(stream, s):
        if isinstance(stream, str) and stream == "text":
            rows = text_hbm.shape[1]
            at = pl.ds(pl.multiple_of(s * rows, rows), rows)
            return text_hbm, tbuf.at[:, at, :], sem_t_s, sem_t_r.at[s]
        if isinstance(stream, str):
            rows = proj_hbm.shape[0]
            at = pl.ds(pl.multiple_of(s * rows, rows), rows)
            return proj_hbm, pbuf.at[at, :], sem_p_s, sem_p_r.at[s]
        rows = w_hbm.shape[1]
        at = pl.ds(pl.multiple_of(s * rows, rows), rows)
        part = pl.ds(pl.multiple_of(stream * width, width), width)
        return w_hbm.at[:, :, part], wbuf.at[stream, :, at, :], sem_w_s.at[stream], sem_w_r.at[stream, s]

    def own_copies(stream):
        src, dst, send, recv = chunk(stream, lon)
        return (
            pltpu.make_async_copy(src, dst, recv),
            remote(src, dst, send.at[0, z], recv, left),
            remote(src, dst, send.at[1, z], recv, right),
            remote(src, dst, send.at[2, z], recv, partner),
        )

    def start_own(stream):
        here, to_left, to_right, to_partner = own_copies(stream)

        @pl.when(z > 0)
        def _():
            to_left.start()

        @pl.when(z < line - 1)
        def _():
            to_right.start()

        to_partner.start()
        here.start()

    def arrived(stream, s):
        _, dst, send, recv = chunk(stream, s)
        return remote(dst, dst, send.at[2, z], recv, partner)

    def pass_on(stream, zz, way, target, more):
        arrived(stream, 2 * zz + core).wait_recv()
        _, dst, send, recv = chunk(stream, 2 * zz + core)

        @pl.when(more)
        def _():
            remote(dst, dst, send.at[way, zz], recv, target).start()

        remote(dst, dst, send.at[2, zz], recv, partner).start()

    def forward(stream, d):
        @pl.when(z + d < line)
        def _():
            pass_on(stream, z + d, 0, left, z > 0)

        @pl.when(z - d >= 0)
        def _():
            pass_on(stream, z - d, 1, right, z < line - 1)

    at_end = (z == 0) | (z == line - 1)

    def relay(*steps):
        @pl.when(jnp.logical_not(at_end))
        def _():
            for stream, d in steps:
                forward(stream, d)

    def take(stream):
        @pl.when(at_end)
        def _():
            for d in range(1, line):
                forward(stream, d)

        wait_all(stream)

    def wait_all(stream):
        own_copies(stream)[0].wait()
        for zz in range(line):
            arrived(stream, 2 * zz + 1 - core).wait_recv()

    def wait_sends(stream):
        for zz in range(line):
            _, dst, send, recv = chunk(stream, 2 * zz + core)

            @pl.when((z > 0) & (zz >= z))
            def _():
                remote(dst, dst, send.at[0, zz], recv, left).wait_send()

            @pl.when((z < line - 1) & (zz <= z))
            def _():
                remote(dst, dst, send.at[1, zz], recv, right).wait_send()

            remote(dst, dst, send.at[2, zz], recv, partner).wait_send()

    slot = core * heads + head

    def plane_copies():
        copies = []
        for k in range(2):
            for j in range(heads):
                if k == 0 and j == 0:
                    continue
                target = (lon if k == 0 else partner[0], other_head(j))
                n = k * heads + j
                copies.append(remote(part_ref, pa.at[slot], sem_pa_s.at[n], sem_pa_r.at[slot], target))
        return copies

    def line_copies():
        return [
            remote(
                mod, pb.at[z], sem_pb_s.at[dz], sem_pb_r.at[z],
                (2 * lax.rem(z + dz, line) + core, head),
            )
            for dz in range(1, line)
        ]

    for copy in plane_copies():
        copy.start()
    start_own(0)
    x_tile = min(128, tokens)
    x_tiles = tokens // x_tile

    def x_copy(i):
        at = pl.ds(pl.multiple_of(i * x_tile, x_tile), x_tile)
        return pltpu.make_async_copy(x_hbm.at[at, :], xm.at[at, :], sem_x.at[i])

    for i in range(x_tiles):
        x_copy(i).start()
    out_cols = img.shape[1]
    col = pl.multiple_of(head * out_cols, out_cols)
    img_copy = pltpu.make_async_copy(x_hbm.at[:, pl.ds(col, out_cols)], img, sem_img)
    img_copy.start()

    pa[slot] = part_ref[...]
    bias_row[...] = proj_bias_ref[...].astype(jnp.float32).reshape(1, depth)

    for k in range(2):
        for j in range(heads):
            if k == 0 and j == 0:
                continue
            there = (core if k == 0 else 1 - core) * heads + other_head(j)
            remote(part_ref, pa.at[there], sem_pa_s.at[0], sem_pa_r.at[there], outer).wait_recv()
    total = pa[0]
    for n in range(1, 2 * heads):
        total = total + pa[n]
    mod[...] = total
    pb[z] = total
    for copy in line_copies():
        copy.start()
    start_own("text")

    block = QROWS * cols
    row_blocks = tokens // block
    side_of_outer = 2 * core - 1
    query = lax.broadcasted_iota(jnp.int32, (block, 3 * block), 0)
    key = lax.broadcasted_iota(jnp.int32, (block, 3 * block), 1)
    row_gap = key // cols - QROWS - query // cols
    for n, side in enumerate((side_of_outer, 0, -side_of_outer)):
        col_gap = key % cols + side * cols - query % cols
        inside = (jnp.abs(row_gap) <= RADIUS) & (jnp.abs(col_gap) <= RADIUS)
        near[n] = jnp.where(inside, 0.0, -1e30).astype(near.dtype)

    for dz in range(1, line):
        zz = lax.rem(z + dz, line)
        remote(mod, pb.at[zz], sem_pb_s.at[0], sem_pb_r.at[zz], outer).wait_recv()
    for copy in line_copies():
        copy.wait_send()
    total = mod_bias_ref[...].astype(jnp.float32)
    for n in range(line):
        total = total + pb[n]
    mod[...] = total

    step_rows = min(32, x_tile)

    def norm_tile(i):
        x_copy(i).wait()

        def one(j, carry):
            at = pl.ds(pl.multiple_of(i * x_tile + j * step_rows, step_rows), step_rows)
            v = xm[at, :].astype(jnp.float32)
            centred = v - jnp.mean(v, axis=1, keepdims=True)
            variance = jnp.mean(centred * centred, axis=1, keepdims=True)
            scaled = (1.0 + mod[1:2, :]) * (centred * lax.rsqrt(variance + 1e-06)) + mod[0:1, :]
            xm[at, :] = scaled.astype(xm.dtype)
            return carry

        lax.fori_loop(0, x_tile // step_rows, one, 0)

    share = tokens // heads

    def share_at(h):
        return pl.ds(pl.multiple_of(h * share, share), share)

    def halo_copy():
        return remote(xm.at[share_at(head), :], xh.at[share_at(head), :], sem_h_s, sem_h_r, outer)

    x_peer, y_peer = head + 1 - 2 * lax.rem(head, 2), head + 2 - 4 * (head // 2)
    half = share // 2

    def spread_copy(part, h, n, target):
        at = pl.ds(pl.multiple_of(h * share + part * half, half), half)
        return remote(
            xh.at[at, :], xh.at[at, :], sem_f_s.at[part, n], sem_f_r.at[part, h], (lon, target)
        )

    def spread_first():
        if heads != 4:
            return [
                spread_copy(part, head, j, other_head(j)) for part in range(2) for j in range(1, heads)
            ]
        return [
            spread_copy(0, head, 1, x_peer),
            spread_copy(1, head, 1, y_peer),
            spread_copy(0, head, 2, y_peer),
            spread_copy(1, head, 2, x_peer),
        ]

    def spread_second():
        if heads != 4:
            return []
        return [spread_copy(0, x_peer, 3, y_peer), spread_copy(1, y_peer, 3, x_peer)]

    def spread():
        halo_copy().wait_recv()
        for copy in spread_first():
            copy.start()

    def spread_on():
        if heads == 4:
            spread_copy(0, x_peer, 0, x_peer).wait_recv()
            spread_copy(1, y_peer, 0, x_peer).wait_recv()
            for copy in spread_second():
                copy.start()

    def wait_halo():
        for j in range(1, heads):
            h = other_head(j)
            for part in range(2):
                if heads == 4:

                    @pl.when(h != (x_peer, y_peer)[part])
                    def _():
                        spread_copy(part, h, 0, x_peer).wait_recv()

                else:
                    spread_copy(part, h, 0, head).wait_recv()

    tile = min(256, tokens)

    def normed(raw, gain_ref):
        pieces = []
        for h in range(width // head_dim):
            entries = raw[:, h * head_dim : (h + 1) * head_dim]
            mean_square = jnp.mean(entries * entries, axis=-1, keepdims=True)
            pieces.append((entries * lax.rsqrt(mean_square + 1e-06) * gain_ref[...]).astype(jnp.bfloat16))
        return pieces

    def product(x_ref, at, g, which):
        raw = jnp.dot(x_ref[at, :], wbuf[g, which], preferred_element_type=jnp.float32)
        part = pl.ds(pl.multiple_of(g * width, width), width)
        return raw + qkv_bias_ref[which : which + 1, part].astype(jnp.float32)

    def put(dst, at, pieces):
        for h, piece in enumerate(pieces):
            dst[at, h * head_dim : (h + 1) * head_dim] = piece

    def project_own(g, i):
        at = pl.ds(pl.multiple_of(i * tile, tile), tile)
        put(kv_own.at[g, 0], at, normed(product(xm, at, g, 1), k_gain_ref))
        kv_own[g, 1, at, :] = product(xm, at, g, 2).astype(jnp.bfloat16)
        put(q_buf, at, normed(product(xm, at, g, 0), q_gain_ref))

    def project_halo(g, i):
        at = pl.ds(pl.multiple_of(i * tile, tile), tile)
        put(kv_outer.at[0], at, normed(product(xh, at, g, 1), k_gain_ref))
        kv_outer[1, at, :] = product(xh, at, g, 2).astype(jnp.bfloat16)

    def kv_copy(g):
        return remote(kv_own.at[g], kv_inner.at[g], sem_kv_s.at[g], sem_kv_r.at[g], partner)

    factor = math.log2(math.e) / math.sqrt(head_dim)
    contract = (((1,), (1,)), ((), ()))

    def attend(g, qb):
        low, high = max(qb - 1, 0), min(qb + 2, row_blocks)
        first = (low - qb + 1) * block
        span = (high - low) * block
        rows_q = slice(qb * block, (qb + 1) * block)
        rows_k = slice(low * block, high * block)

        def one_head(hh, carry):
            lanes = pl.ds(pl.multiple_of(hh * head_dim, head_dim), head_dim)
            text_lanes = pl.ds(pl.multiple_of(g * width + hh * head_dim, head_dim), head_dim)
            q = q_buf[rows_q, lanes]
            scores = []
            values = []
            for n, kv in enumerate((kv_outer, kv_own.at[g], kv_inner.at[g])):
                s = lax.dot_general(q, kv[0, rows_k, lanes], contract, preferred_element_type=jnp.float32)
                scores.append(s + near[n, :, first : first + span])
                values.append(kv[1, rows_k, lanes])
            scores.append(
                lax.dot_general(q, tbuf[0, :, text_lanes], contract, preferred_element_type=jnp.float32)
            )
            values.append(tbuf[1, :, text_lanes])
            highest = functools.reduce(
                jnp.maximum, [jnp.max(s, axis=1, keepdims=True) for s in scores]
            )
            total = 0.0
            out = 0.0
            for s, v in zip(scores, values):
                p = jnp.exp2((s - highest) * factor)
                total = total + jnp.sum(p, axis=1, keepdims=True)
                out = out + jnp.dot(p.astype(jnp.bfloat16), v, preferred_element_type=jnp.float32)
            ag[head, rows_q, text_lanes] = (out / total).astype(ag.dtype)
            return carry

        lax.fori_loop(0, width // head_dim, one_head, 0)

    far = heads - 1 - head

    def share_copy(h, g, qb, part, recv, send, target):
        rows = block if part is None else block // 2
        first = qb * block + (0 if part is None else part * rows)
        piece = ag.at[
            h, pl.ds(pl.multiple_of(first, rows), rows), pl.ds(pl.multiple_of(g * width, width), width)
        ]
        n = g * row_blocks + qb
        return remote(piece, piece, sem_a_s.at[send, n], sem_a_r.at[recv, n], (lon, target))

    def share_copies(g, qb):
        if heads != 4:
            return [
                share_copy(head, g, qb, None, head, j, other_head(j)) for j in range(1, heads)
            ]
        return [
            share_copy(head, g, qb, None, head, 0, x_peer),
            share_copy(head, g, qb, None, head, 1, y_peer),
        ]

    def passed_copies(g, qb):
        if heads != 4:
            return []
        return [
            share_copy(x_peer, g, qb, 0, x_peer, 2, y_peer),
            share_copy(y_peer, g, qb, 1, heads, 3, x_peer),
        ]

    def pass_shares(g, qb):
        if heads == 4:
            for h in (x_peer, y_peer):
                share_copy(h, g, qb, None, h, 0, x_peer).wait_recv()
            for copy in passed_copies(g, qb):
                copy.start()

    def wait_shares(g, qb):
        if heads == 4:
            share_copy(far, g, qb, 0, far, 0, x_peer).wait_recv()
            share_copy(far, g, qb, 1, heads, 0, x_peer).wait_recv()
        else:
            for j in range(1, heads):
                share_copy(other_head(j), g, qb, None, other_head(j), 0, head).wait_recv()

    tiles = tokens // tile
    lag = 2

    def norm_step(i, carry):
        norm_tile(i)
        return carry

    relay((0, 1))
    lax.fori_loop(0, x_tiles, norm_step, 0)
    halo_copy().start()
    relay(("text", 1))
    relay(*[(stream, d) for d in range(2, line) for stream in (0, "text")])
    start_own(1)
    relay((1, 1))
    start_own(2)

    @pl.when(at_end)
    def _():
        start_own("proj")

    spread()
    take(0)

    def group_step(g, carry):
        @pl.when(g > 0)
        def _():
            take(g)

        def own_step(i, carry):
            project_own(g, i)

            for late in range(lag):

                @pl.when((g > 0) & (i == late * tiles // lag))
                def _():
                    pass_shares(g - 1, row_blocks - lag + late)

            @pl.when((g == 1) & (i == 1))
            def _():
                relay(("proj", 1))

            @pl.when((g == 2) & (i == 1))
            def _():
                relay(*[("proj", d) for d in range(2, line)])

            return carry

        lax.fori_loop(0, tiles, own_step, 0)
        kv_copy(g).start()

        @pl.when(g == 0)
        def _():
            spread_on()
            relay(*[(1, d) for d in range(2, line)])
            relay((2, 1))
            wait_halo()

        def halo_step(i, carry):
            project_halo(g, i)
            return carry

        lax.fori_loop(0, tiles, halo_step, 0)

        @pl.when(g == 0)
        def _():
            take("text")

        kv_copy(g).wait_recv()
        for qb in range(row_blocks):
            attend(g, qb)
            for copy in share_copies(g, qb):
                copy.start()
            if qb >= lag:
                pass_shares(g, qb - lag)
            if qb == 1:

                @pl.when((g == 0) & jnp.logical_not(at_end))
                def _():
                    relay(*[(2, d) for d in range(2, line)])
                    start_own("proj")
        return carry

    lax.fori_loop(0, groups, group_step, 0)
    for late in range(lag):
        pass_shares(groups - 1, row_blocks - lag + late)

    take("proj")
    img_copy.wait()
    gate = mod[2:3, pl.ds(col, out_cols)]

    def out_copy(qb):
        at = pl.ds(pl.multiple_of(qb * block, block), block)
        return pltpu.make_async_copy(img.at[at, :], out_hbm.at[at, :], sem_out.at[qb])

    def out_step(qb, carry):
        for g in range(groups):
            wait_shares(g, qb)
        rows = pl.ds(pl.multiple_of(qb * block, block), block)
        total = bias_row[:, pl.ds(col, out_cols)]
        for k in range(heads):
            total = total + jnp.dot(
                ag[k, rows, :], pbuf[k * inner : (k + 1) * inner, :], preferred_element_type=jnp.float32
            )
        img[rows, :] = (img[rows, :].astype(jnp.float32) + gate * total).astype(img.dtype)
        out_copy(qb).start()
        return carry

    lax.fori_loop(0, row_blocks, out_step, 0)

    for copy in plane_copies():
        copy.wait_send()
    wait_sends("text")
    wait_sends("proj")

    def sent_step(g, carry):
        wait_sends(g)
        kv_copy(g).wait_send()
        for qb in range(row_blocks):
            for copy in share_copies(g, qb) + passed_copies(g, qb):
                copy.wait_send()
        return carry

    lax.fori_loop(0, groups, sent_step, 0)
    halo_copy().wait_send()
    for copy in spread_first() + spread_second():
        copy.wait_send()
    for qb in range(row_blocks):
        out_copy(qb).wait()


def body(
    image_tokens,
    conditioning,
    mod_weight,
    mod_bias,
    qkv_weight,
    qkv_bias,
    q_gain,
    k_gain,
    text_kv,
    proj_weight,
    proj_bias,
):
    lat_rows, cols, depth = image_tokens.shape
    tokens = lat_rows * cols
    lons, heads = lax.axis_size("lon"), lax.axis_size("head")
    line = lons // 2
    rows, _, inner = qkv_weight.shape
    head_dim = q_gain.shape[0]
    groups = 3
    width = inner // groups
    text_rows = text_kv.shape[1]
    out_cols = proj_weight.shape[1]
    block = QROWS * cols
    row_blocks = tokens // block

    w = qkv_weight.transpose(1, 0, 2)

    slice_rows = mod_weight.shape[0]
    first = (lax.axis_index("lon") * heads + lax.axis_index("head")) * slice_rows
    silu_part = jax.nn.silu(
        lax.dynamic_slice_in_dim(conditioning, first, slice_rows, 0).astype(jnp.float32)
    )
    part = jnp.dot(
        silu_part,
        mod_weight.reshape(slice_rows, 3 * depth).astype(jnp.float32),
        precision=lax.Precision.HIGHEST,
    ).reshape(3, depth)
    x_tiles = tokens // min(128, tokens)
    vmem = pl.BlockSpec(memory_space=pltpu.VMEM)
    anywhere = pl.BlockSpec(memory_space=pl.ANY)
    dma = pltpu.SemaphoreType.DMA
    out = pl.pallas_call(
        functools.partial(kernel, (lons, heads, cols, head_dim)),
        out_shape=jax.ShapeDtypeStruct((tokens, out_cols), jnp.bfloat16),
        in_specs=[anywhere, vmem, vmem, anywhere, vmem, vmem, vmem, anywhere, anywhere, vmem],
        out_specs=anywhere,
        scratch_shapes=[
            pltpu.VMEM((tokens, depth), jnp.bfloat16),
            pltpu.VMEM((tokens, depth), jnp.bfloat16),
            pltpu.VMEM((groups, 3, depth, width), jnp.bfloat16),
            pltpu.VMEM((heads * inner, out_cols), jnp.bfloat16),
            pltpu.VMEM((2, lons * text_rows, inner), jnp.bfloat16),
            pltpu.VMEM((groups, 2, tokens, width), jnp.bfloat16),
            pltpu.VMEM((groups, 2, tokens, width), jnp.bfloat16),
            pltpu.VMEM((2, tokens, width), jnp.bfloat16),
            pltpu.VMEM((tokens, width), jnp.bfloat16),
            pltpu.VMEM((heads, tokens, inner), jnp.bfloat16),
            pltpu.VMEM((tokens, out_cols), jnp.bfloat16),
            pltpu.VMEM((3, block, 3 * block), jnp.float32),
            pltpu.VMEM((2 * heads, 3, depth), jnp.float32),
            pltpu.VMEM((line, 3, depth), jnp.float32),
            pltpu.VMEM((3, depth), jnp.float32),
            pltpu.VMEM((1, depth), jnp.float32),
            dma((2 * heads,)),
            dma((2 * heads,)),
            dma((line,)),
            dma((line,)),
            dma((groups, 3, line)),
            dma((groups, lons)),
            dma((3, line)),
            dma((lons,)),
            dma((3, line)),
            dma((lons,)),
            dma,
            dma,
            dma((2, heads)),
            dma((2, heads)),
            dma((groups,)),
            dma((groups,)),
            dma((heads, groups * row_blocks)),
            dma((heads + 1, groups * row_blocks)),
            dma((x_tiles,)),
            dma,
            dma((row_blocks,)),
        ],
        compiler_params=pltpu.CompilerParams(
            collective_id=0, has_side_effects=True, vmem_limit_bytes=VMEM_LIMIT
        ),
        cost_estimate=pl.CostEstimate(
            flops=2 * tokens * depth * inner * 6, bytes_accessed=8 * tokens * depth, transcendentals=0
        ),
    )(
        image_tokens.reshape(tokens, depth),
        part,
        mod_bias,
        w,
        qkv_bias,
        q_gain.reshape(1, head_dim),
        k_gain.reshape(1, head_dim),
        text_kv,
        proj_weight,
        proj_bias,
    )
    return out.reshape(lat_rows, cols, out_cols)


def solution(mesh):
    placed = (
        P(None, "lon", None),
        P(),
        P(("lon", "head"), None, None),
        P(),
        P("lon", None, "head"),
        P(None, "head"),
        P(),
        P(),
        P(None, "lon", "head"),
        P("lon", "head"),
        P(),
    )
    return jax.shard_map(
        body, mesh=mesh, in_specs=placed, out_specs=P(None, "lon", "head"), check_vma=False
    )
```
